1024 devices in a mesh: row: 32 (over x_hi, z), col: 32 (over x_lo, y, core).
Axes of the slice: x: 4 (x_hi: 2, x_lo: 2; x = x_hi * 2 + x_lo), y: 8, z: 16, core: 2. Of those that a mesh axis runs over, the one named last changes fastest.
Arguments:
- queries: bfloat16 [256, 512, 768], P('row', 'col'), may hold values from -6 to 6
- keys: bfloat16 [256, 512, 768], P('row', 'col'), may hold values from -6 to 6
- values: bfloat16 [256, 512, 768], P('row', 'col'), may hold values from -6 to 6
- d_out: bfloat16 [256, 512, 768], P('row', 'col'), may hold values from -6 to 6
- extents: int32 [2, 16, 32], replicated, may hold values from 4 to 16, as said below
- rel_bias: float32 [12, 13, 13], replicated, may hold values from -4 to 4
Outputs:
- attended: bfloat16 [256, 512, 768], P('row', 'col')
- d_queries: bfloat16 [256, 512, 768], P('row', 'col')
- d_keys: bfloat16 [256, 512, 768], P('row', 'col')
- d_values: bfloat16 [256, 512, 768], P('row', 'col')
- d_rel_bias: float32 [12, 13, 13], replicated
The draws below stay inside these ranges and needn't reach their ends.
Inputs may be any that keep to these rules, and one draw needn't show every extreme that they name: `extents`: every slot holds one image at its top-left corner.
All inputs are finite; a program needn't handle non-finite values.
Results may differ from the reference program's by a relative error of at most 0.011.
Values may be sent and summed in bfloat16 or wider, within the bound.
No kernel may reach another device: no remote copies, remote signals or barrier semaphores. Data moves between devices by JAX's collectives and lax.ppermute only.
A program may use at most 64 MiB of HBM per device.

```python
import jax
import jax.numpy as jnp
from jax import lax

HEADS = 12
HDIM = 64
RAD = 6
GROUP = 4
TH = 8
TW = 16
WIDTH = 768
SPAN = 13
IH = 256
IW = 512
PANEL = 16
PR = 16
PC = 32
N_ROW = 32
N_COL = 32


def drawn_pair(key):
    base = jax.random.fold_in(key, 17)
    key_q, key_k = jax.random.split(base, 2)
    shape = (IH, IW, HEADS * HDIM)
    queries = jnp.clip(jax.random.normal(key_q, shape, jnp.float32), -6.0, 6.0)
    keys = jnp.clip(jax.random.normal(key_k, shape, jnp.float32), -6.0, 6.0)
    return (queries, keys)


def draw_queries(key, part):
    return drawn_pair(key)[0].astype(jnp.bfloat16)


def draw_keys(key, part):
    return drawn_pair(key)[1].astype(jnp.bfloat16)


def draw_extents(key, part):
    key_h, key_w = jax.random.split(jax.random.fold_in(key, 29))
    heights = jax.random.randint(key_h, (PR, PC), PANEL // 4, PANEL + 1)
    widths = jax.random.randint(key_w, (PR, PC), PANEL // 4, PANEL + 1)
    heights = heights.at[0, 0].set(PANEL).at[PR - 1, PC - 1].set(PANEL // 4)
    widths = widths.at[0, 0].set(PANEL).at[PR - 1, PC - 1].set(PANEL // 4)
    return jnp.stack([heights, widths]).astype(jnp.int32)


def block_levels(key, shape, cuts, smallest, largest):
    loudness = 1.0
    for position, parts in cuts:
        steps = jax.random.uniform(jax.random.fold_in(jax.random.fold_in(key, 6), position), (parts,), jnp.float32, smallest / len(cuts), largest / len(cuts))
        loudness = loudness * jnp.repeat(jnp.exp(steps), shape[position] // parts).reshape((-1,) + (1,) * (len(shape) - 1 - position))
    return loudness


def noise(key, dims, deviation, reach, shards=(), kind=jnp.bfloat16):
    level = block_levels(key, dims, shards, -0.22, 0.18) if shards else 1.0
    array = jax.random.normal(key, dims, jnp.float32) * deviation * level
    return jnp.minimum(jnp.maximum(array, -reach), reach).astype(kind)


def setup_inputs(seed: int = 0) -> dict:
    key_list = jax.random.split(jax.random.key(seed), 7)
    return {
        "queries": draw_queries(jax.random.fold_in(key_list[6], 71), 0),
        "keys": draw_keys(jax.random.fold_in(key_list[6], 71), 0),
        "values": noise(key_list[2], (IH, IW, WIDTH), 1.0, 6.0, ((0, 32), (1, 32))),
        "d_out": noise(key_list[3], (IH, IW, WIDTH), 1.0, 6.0, ((0, 32), (1, 32))),
        "extents": draw_extents(jax.random.fold_in(key_list[6], 71), 0),
        "rel_bias": noise(key_list[5], (HEADS, SPAN, SPAN), 1.0, 4.0, (), jnp.float32),
    }


HIGH = lax.Precision.HIGHEST


def offset_tables(group_rows, tile_cols, radius):
    span_size = 2 * radius + 1
    query_rows = jnp.arange(group_rows, dtype=jnp.int32)
    key_rows = jnp.arange(group_rows + 2 * radius, dtype=jnp.int32)
    row_offsets = ((key_rows[None, :] - query_rows[:, None])[:, :, None] == jnp.arange(span_size, dtype=jnp.int32)[None, None, :]).astype(jnp.float32)
    query_cols = jnp.arange(tile_cols, dtype=jnp.int32)
    key_cols = jnp.arange(tile_cols + 2 * radius, dtype=jnp.int32)
    col_offsets = ((key_cols[None, :] - query_cols[:, None])[:, :, None] == jnp.arange(span_size, dtype=jnp.int32)[None, None, :]).astype(jnp.float32)
    return row_offsets, col_offsets


def canvas_valid(extents):
    rows = jnp.arange(IH, dtype=jnp.int32)
    cols = jnp.arange(IW, dtype=jnp.int32)
    heights = extents[0][rows // PANEL][:, cols // PANEL]
    widths = extents[1][rows // PANEL][:, cols // PANEL]
    return ((rows % PANEL)[:, None] < heights) & ((cols % PANEL)[None, :] < widths)


def offset_sum(dscore, row_offsets, col_offsets):
    head_count = dscore.shape[0]
    group_rows, band_rows = row_offsets.shape[0], row_offsets.shape[1]
    tile_cols, band_cols = col_offsets.shape[0], col_offsets.shape[1]
    shaped = dscore.reshape(head_count, group_rows, tile_cols, band_rows, band_cols)
    by_col = jnp.einsum("hicjm,cmb->hijb", shaped, col_offsets, precision=HIGH)
    return jnp.einsum("hijb,ija->hab", by_col, row_offsets, precision=HIGH)


def tile_pass(query_tile, grad_tile, band, band_valid, bias, window, row_offsets, col_offsets):
    tile_rows, tile_cols, channels = query_tile.shape
    head_count = bias.shape[0]
    head_size = channels // head_count
    scale = head_size ** -0.5
    band_cols = band.shape[2]
    radius = (band_cols - tile_cols) // 2
    band_rows = GROUP + 2 * radius
    out_pieces = []
    dq_pieces = []
    grads = jnp.zeros((2, band.shape[1], band_cols, channels), jnp.float32)
    bias_grad = jnp.zeros((head_count, row_offsets.shape[2], col_offsets.shape[2]), jnp.float32)
    for block in range(tile_rows // GROUP):
        first = block * GROUP
        query_heads = query_tile[first:first + GROUP].reshape(GROUP * tile_cols, head_count, head_size).astype(jnp.float32)
        key_heads = band[0, first:first + band_rows].reshape(band_rows * band_cols, head_count, head_size).astype(jnp.float32)
        value_heads = band[1, first:first + band_rows].reshape(band_rows * band_cols, head_count, head_size).astype(jnp.float32)
        valid_query = band_valid[first + radius:first + radius + GROUP, radius:radius + tile_cols].reshape(-1)
        valid_key = band_valid[first:first + band_rows].reshape(-1)
        allowed = window & valid_query[:, None] & valid_key[None, :]
        score = jnp.einsum("qhd,khd->hqk", query_heads, key_heads, precision=HIGH) * scale + bias
        score = jnp.where(allowed[None], score, -1e30)
        highest = jnp.max(score, axis=-1, keepdims=True)
        weights = jnp.exp(score - highest)
        prob = weights / jnp.sum(weights, axis=-1, keepdims=True)
        prob_b = lax.optimization_barrier(prob.astype(jnp.bfloat16)).astype(jnp.float32)
        output = jnp.einsum("hqk,khd->qhd", prob_b, value_heads, precision=HIGH)
        out_pieces.append(jnp.where(valid_query[:, None, None], output, 0.0).astype(jnp.bfloat16).reshape(GROUP, tile_cols, channels))
        grad_rows = grad_tile[first:first + GROUP].reshape(GROUP * tile_cols, head_count, head_size).astype(jnp.float32)
        grad_heads = jnp.where(valid_query[:, None, None], grad_rows, 0.0)
        delta = jnp.sum(grad_heads * output, axis=-1)
        dprob = jnp.einsum("qhd,khd->hqk", grad_heads, value_heads, precision=HIGH)
        dscore = prob * (dprob - jnp.transpose(delta)[:, :, None])
        dscore_b = lax.optimization_barrier(dscore.astype(jnp.bfloat16)).astype(jnp.float32)
        dq_block = jnp.einsum("hqk,khd->qhd", dscore_b, key_heads, precision=HIGH) * scale
        dq_pieces.append(dq_block.astype(jnp.bfloat16).reshape(GROUP, tile_cols, channels))
        dk_block = jnp.einsum("hqk,qhd->khd", dscore_b, query_heads, precision=HIGH) * scale
        dv_block = jnp.einsum("hqk,qhd->khd", prob_b, grad_heads, precision=HIGH)
        grads = grads.at[:, first:first + band_rows].add(jnp.stack([dk_block, dv_block]).reshape(2, band_rows, band_cols, channels))
        bias_grad = bias_grad + offset_sum(dscore, row_offsets, col_offsets)
    return jnp.concatenate(out_pieces, 0), jnp.concatenate(dq_pieces, 0), grads, bias_grad


def reference(queries, keys, values, d_out, extents, rel_bias):
    channels = HEADS * HDIM
    band_rows = GROUP + 2 * RAD
    band_cols = TW + 2 * RAD
    row_offsets, col_offsets = offset_tables(GROUP, TW, RAD)
    bias = jnp.einsum("hab,ija,cmb->hicjm", rel_bias.astype(jnp.float32), row_offsets, col_offsets, precision=HIGH).reshape(HEADS, GROUP * TW, band_rows * band_cols)
    window = (jnp.sum(row_offsets, -1)[:, None, :, None] * jnp.sum(col_offsets, -1)[None, :, None, :] > 0.5).reshape(GROUP * TW, band_rows * band_cols)
    valid = jnp.pad(canvas_valid(extents), RAD)
    band_all = jnp.pad(jnp.stack([keys, values]), ((0, 0), (RAD, RAD), (RAD, RAD), (0, 0)))
    zero = jnp.zeros((), jnp.int32)

    def step(carry, index):
        accum, bias_total = carry
        row_start = ((index // N_COL) * TH).astype(jnp.int32)
        col_start = ((index % N_COL) * TW).astype(jnp.int32)
        query_tile = lax.dynamic_slice(queries, (row_start, col_start, zero), (TH, TW, channels))
        grad_tile = lax.dynamic_slice(d_out, (row_start, col_start, zero), (TH, TW, channels))
        band = lax.dynamic_slice(band_all, (zero, row_start, col_start, zero), (2, TH + 2 * RAD, band_cols, channels))
        band_valid = lax.dynamic_slice(valid, (row_start, col_start), (TH + 2 * RAD, band_cols))
        out_tile, dq_tile, grads, bias_part = tile_pass(query_tile, grad_tile, band, band_valid, bias, window, row_offsets, col_offsets)
        older = lax.dynamic_slice(accum, (zero, row_start, col_start, zero), grads.shape)
        accum = lax.dynamic_update_slice(accum, older + grads, (zero, row_start, col_start, zero))
        return (accum, bias_total + bias_part), (out_tile, dq_tile)

    start = (jnp.zeros((2, IH + 2 * RAD, IW + 2 * RAD, channels), jnp.float32), jnp.zeros((HEADS, 2 * RAD + 1, 2 * RAD + 1), jnp.float32))
    (accum, bias_total), (out_tiles, dq_tiles) = lax.scan(step, start, jnp.arange(N_ROW * N_COL, dtype=jnp.int32))

    def assemble(tiles):
        return jnp.transpose(tiles.reshape(N_ROW, N_COL, TH, TW, channels), (0, 2, 1, 3, 4)).reshape(IH, IW, channels)

    d_keys = accum[0, RAD:RAD + IH, RAD:RAD + IW].astype(jnp.bfloat16)
    d_values = accum[1, RAD:RAD + IH, RAD:RAD + IW].astype(jnp.bfloat16)
    return (assemble(out_tiles), assemble(dq_tiles), d_keys, d_values, bias_total)
```

```python
import functools

import jax
import jax.numpy as jnp
from jax import lax
from jax.experimental import pallas as pl
from jax.experimental.pallas import tpu as pltpu
from jax.sharding import PartitionSpec as P

NEG = -1e30
HIGH = lax.Precision.HIGHEST
NT = (((1,), (1,)), ((), ()))
TN = (((0,), (0,)), ((), ()))
NN = (((1,), (0,)), ((), ()))

ROWS = 20
SLOTS = 32
OWN = 16
EDGE = 8
RAD = 6
SPAN = 13
TILE = 128


def dot(a, b, dims, precision=None):
    return lax.dot_general(a, b, dims, precision=precision, preferred_element_type=jnp.float32)


def iota(shape, dim):
    return lax.broadcasted_iota(jnp.int32, shape, dim)


def slot_offset():
    slot = iota((SLOTS, TILE), 0)
    lane = iota((SLOTS, TILE), 1)
    column = jnp.where(
        slot < OWN, slot + RAD, jnp.where(slot < OWN + EDGE, slot - OWN - EDGE + RAD, slot - EDGE + RAD)
    )
    return column - (lane & 15), lane >> 4


def row_pick(dim):
    shape = (16, 2 * TILE)
    lane = iota(shape, 1)
    offset = ((8 - ((lane >> 4) & 7)) & 7) + 8 * (lane >> 7)
    return (iota(shape, 0) == offset).astype(jnp.float32)


def bias_body(ext_ref, table_ref, out_ref, mask_ref):
    offset, query_row = slot_offset()

    @pl.when(pl.program_id(0) == 0)
    def _():
        row, col = lax.axis_index("row"), lax.axis_index("col")
        last_row, last_col = ext_ref.shape[1] - 1, ext_ref.shape[2] - 1
        slot = iota((SLOTS, TILE), 0)
        lane = iota((SLOTS, TILE), 1)
        panel = row // 2
        valid_query = ((row % 2) * 8 + query_row < ext_ref[0, panel, col]) & (
            (lane & 15) < ext_ref[1, panel, col]
        )
        near = valid_query & (offset >= 0) & (offset < SPAN)
        local = jnp.where(slot < OWN, slot, jnp.where(slot < OWN + EDGE, slot - EDGE, slot - OWN - EDGE))
        for j in range(ROWS):
            r = row * 8 + (j - RAD + 16)
            panel_row = r // 16 - 1
            inside_row = (panel_row >= 0) & (panel_row <= last_row)
            panel_row = jnp.minimum(jnp.maximum(panel_row, 0), last_row)
            widths = []
            for step in (0, -1, 1):
                at = col + step
                inside = inside_row & (at >= 0) & (at <= last_col)
                at = jnp.minimum(jnp.maximum(at, 0), last_col)
                tall = inside & (r % 16 < ext_ref[0, panel_row, at])
                widths.append(jnp.where(tall, ext_ref[1, panel_row, at], 0))
            width = jnp.where(slot < OWN, widths[0], jnp.where(slot < OWN + EDGE, widths[1], widths[2]))
            allowed = near & (local < width) & (query_row <= j) & (query_row >= j - SPAN + 1)
            mask_ref[j * SLOTS : (j + 1) * SLOTS, :] = jnp.where(allowed, 0.0, NEG)

    spread = dot(table_ref[0], row_pick(0), NN, HIGH)
    low = jnp.zeros((SLOTS, TILE), jnp.float32)
    high = jnp.zeros((SLOTS, TILE), jnp.float32)
    for b in range(SPAN):
        low = jnp.where(offset == b, spread[b : b + 1, :TILE], low)
        high = jnp.where(offset == b, spread[b : b + 1, TILE:], high)
    for turn in range(8):
        low_turned = pltpu.roll(low, 16 * turn, 1) if turn else low
        high_turned = pltpu.roll(high, 16 * turn, 1) if turn else high
        for j in (turn, turn + 8, turn + 16):
            if j >= ROWS:
                continue
            value = low_turned if j < 8 else high_turned
            if 8 <= j < 15:
                value = jnp.where(query_row > j - 8, low_turned, high_turned)
            at = slice(j * SLOTS, (j + 1) * SLOTS)
            out_ref[0, at, :] = value + mask_ref[at, :]


def attend_body(
    ext_ref, bias_ref, q_ref, g_ref, k_ref, v_ref, t_ref, b_ref, l_ref, r_ref, lc_ref, rc_ref,
    out_ref, dq_ref, own_ref, top_ref, bottom_ref, left_ref, right_ref, part_ref,
    kw_ref, vw_ref, sum_ref,
):
    pair = pl.program_id(0)
    for n, (own, window) in enumerate(((k_ref, kw_ref), (v_ref, vw_ref))):
        window[0:6, 0:16] = t_ref[n]
        window[6:14, 0:16] = own[...]
        window[14:20, 0:16] = b_ref[n]
        window[0:6, 16:24] = lc_ref[n, 0:6]
        window[6:14, 16:24] = l_ref[n]
        window[14:20, 16:24] = lc_ref[n, 6:12]
        window[0:6, 24:32] = rc_ref[n, 0:6]
        window[6:14, 24:32] = r_ref[n]
        window[14:20, 24:32] = rc_ref[n, 6:12]
    keys = kw_ref[...].reshape(ROWS * SLOTS, TILE)
    values = vw_ref[...].reshape(ROWS * SLOTS, TILE)

    row, col = lax.axis_index("row"), lax.axis_index("col")
    panel = row // 2
    token = iota((TILE, TILE), 0)
    valid = ((row % 2) * 8 + (token >> 4) < ext_ref[0, panel, col]) & (
        (token & 15) < ext_ref[1, panel, col]
    )
    first = iota((TILE, TILE), 1) < 64
    queries = q_ref[...].reshape(TILE, TILE).astype(jnp.float32) * 0.125
    grads = jnp.where(valid, g_ref[...].reshape(TILE, TILE).astype(jnp.float32), 0.0)

    def apart(x):
        return jnp.concatenate([jnp.where(first, x, 0.0), jnp.where(first, 0.0, x)], 0)

    grads_f = apart(grads)
    queries_b = apart(queries).astype(jnp.bfloat16)
    grads_b = grads_f.astype(jnp.bfloat16)

    score = dot(keys, queries_b, NT)
    score = score + jnp.concatenate([bias_ref[0], bias_ref[1]], 1)
    highest = jnp.max(score, axis=0, keepdims=True)
    weights = jnp.exp(score - highest)
    prob = weights * (1.0 / jnp.sum(weights, axis=0, keepdims=True))
    prob_b = prob.astype(jnp.bfloat16)
    output = dot(values, prob_b, TN)
    delta = jnp.sum(jnp.transpose(grads_f) * output, axis=0, keepdims=True)
    dprob = dot(values, grads_b, NT)
    dscore = prob * (dprob - delta)
    dscore_b = dscore.astype(jnp.bfloat16)

    head_row = iota((TILE, TILE), 0) < 64

    def together(x):
        return jnp.transpose(jnp.where(head_row, x[:, :TILE], x[:, TILE:]))

    attended = jnp.where(valid, together(output), 0.0)
    out_ref[...] = attended.astype(jnp.bfloat16).reshape(8, 16, TILE)
    dq = together(dot(keys, dscore_b, TN)) * 0.125
    dq_ref[...] = dq.astype(jnp.bfloat16).reshape(8, 16, TILE)
    dk = dot(dscore_b, queries_b, NN)
    dv = dot(prob_b, grads_b, NN)
    for n, grad in enumerate((dk, dv)):
        grad = grad.reshape(ROWS, SLOTS, TILE)
        top_ref[n] = grad[0:6, 0:16]
        own_ref[n] = grad[6:14, 0:16]
        bottom_ref[n] = grad[14:20, 0:16]
        left_ref[n] = grad[:, 16:24].astype(jnp.bfloat16)
        right_ref[n] = grad[:, 24:32].astype(jnp.bfloat16)

    @pl.when(pair == 0)
    def _():
        sum_ref[...] = jnp.zeros_like(sum_ref)

    offset, query_row = slot_offset()
    for head in range(2):
        part = dscore[:, head * TILE : (head + 1) * TILE]
        low = jnp.zeros((SLOTS, TILE), jnp.float32)
        high = jnp.zeros((SLOTS, TILE), jnp.float32)

        def line(j, part=part):
            return part[j * SLOTS : (j + 1) * SLOTS]

        for turn in range(8):
            x = line(turn)
            y = line(turn + 8)
            if turn < 7:
                x = x + jnp.where(query_row > turn, y, 0.0)
                y = jnp.where(query_row > turn, 0.0, y)
            if turn + 16 < ROWS:
                y = y + line(turn + 16)
            back = (TILE - 16 * turn) % TILE
            low = low + (pltpu.roll(x, back, 1) if turn else x)
            high = high + (pltpu.roll(y, back, 1) if turn else y)
        for b in range(SPAN):
            hit = offset == b
            sum_ref[2 * pair + head, b : b + 1, :TILE] = jnp.sum(
                jnp.where(hit, low, 0.0), axis=0, keepdims=True
            )
            sum_ref[2 * pair + head, b : b + 1, TILE:] = jnp.sum(
                jnp.where(hit, high, 0.0), axis=0, keepdims=True
            )

    @pl.when(pair == pl.num_programs(0) - 1)
    def _():
        pick = row_pick(0)
        for half in range(2):
            sums = sum_ref[half * 8 : half * 8 + 8].reshape(TILE, 2 * TILE)
            part_ref[half * 16 : half * 16 + 16, :] = dot(pick, sums, NT, HIGH)


def border_body(top_ref, bottom_ref, fl_ref, fr_ref, up_ref, down_ref):
    for source, rows, target in ((top_ref, slice(0, 6), up_ref), (bottom_ref, slice(14, 20), down_ref)):
        for n in range(2):
            low = source[n, :, :EDGE] + fl_ref[n, rows].astype(jnp.float32)
            high = source[n, :, EDGE:] + fr_ref[n, rows].astype(jnp.float32)
            target[n] = jnp.concatenate([low, high], 1).astype(jnp.bfloat16)


def final_body(own_ref, fl_ref, fr_ref, fu_ref, fd_ref, part_ref, dk_ref, dv_ref, bias_ref):
    for n, target in enumerate((dk_ref, dv_ref)):
        for r in range(8):
            left = own_ref[n, r, :EDGE] + fl_ref[n, r + RAD].astype(jnp.float32)
            right = own_ref[n, r, EDGE:] + fr_ref[n, r + RAD].astype(jnp.float32)
            total = jnp.concatenate([left, right], 0)
            if r < RAD:
                total = total + fu_ref[n, r].astype(jnp.float32)
            if r >= 8 - RAD:
                total = total + fd_ref[n, r - 8 + RAD].astype(jnp.float32)
            target[r] = total.astype(jnp.bfloat16)
    for h in range(bias_ref.shape[0]):
        at = (h % 8) * 16
        bias_ref[h] = part_ref[(h // 8) * 16 : (h // 8) * 16 + SPAN, at : at + SPAN]


def neighbour(value, axis, step):
    size = lax.axis_size(axis)
    return lax.ppermute(value, axis, [(i, i + step) for i in range(size) if 0 <= i + step < size])


def exchange(value, axis):
    return lax.all_to_all(value, axis, 0, 0)


def gathered(piece, axis):
    return exchange(jnp.broadcast_to(piece, (lax.axis_size(axis),) + piece.shape), axis)


def shape(dims, dtype=jnp.bfloat16):
    return jax.ShapeDtypeStruct(dims, dtype)


SMEM = pl.BlockSpec(memory_space=pltpu.SMEM)
VMEM = pl.BlockSpec(memory_space=pltpu.VMEM)


def shards(queries, keys, values, d_out, extents, rel_bias):
    heads = rel_bias.shape[0]
    width = queries.shape[2]
    both = jnp.stack([keys, values])
    top = neighbour(both[:, 2:], "row", 1)
    bottom = neighbour(both[:, :6], "row", -1)
    left = neighbour(both[:, :, EDGE:], "col", 1)
    right = neighbour(both[:, :, :EDGE], "col", -1)

    table = jnp.pad(jnp.swapaxes(rel_bias, 1, 2), ((0, 0), (0, 3), (0, 3)))
    bias = pl.pallas_call(
        bias_body,
        grid=(heads,),
        out_shape=shape((heads, ROWS * SLOTS, TILE), jnp.float32),
        in_specs=[SMEM, pl.BlockSpec((1, 16, 16), lambda h: (h, 0, 0))],
        out_specs=pl.BlockSpec((1, ROWS * SLOTS, TILE), lambda h: (h, 0, 0)),
        scratch_shapes=[pltpu.VMEM((ROWS * SLOTS, TILE), jnp.float32)],
        cost_estimate=pl.CostEstimate(flops=20_000_000, bytes_accessed=4_000_000, transcendentals=0),
        name="bias_mask",
    )(extents, table)

    top, bottom, left, right, bias = lax.optimization_barrier((top, bottom, left, right, bias))
    ends = jnp.concatenate([top, bottom], 1)
    left_ends = neighbour(ends[:, :, EDGE:], "col", 1)
    right_ends = neighbour(ends[:, :, :EDGE], "col", -1)

    def lanes(*dims):
        return pl.BlockSpec(dims + (TILE,), lambda g: (0,) * len(dims) + (g,))

    tile = lanes(8, 16)
    rows_spec, edge_spec, ends_spec = lanes(2, 6, 16), lanes(2, 8, EDGE), lanes(2, 12, EDGE)
    side_spec = lanes(2, ROWS, EDGE)
    attended, d_queries, own, d_top, d_bottom, d_left, d_right, part = pl.pallas_call(
        attend_body,
        grid=(width // TILE,),
        out_shape=(
            shape(queries.shape),
            shape(queries.shape),
            shape((2, 8, 16, width), jnp.float32),
            shape((2, 6, 16, width), jnp.float32),
            shape((2, 6, 16, width), jnp.float32),
            shape((2, ROWS, EDGE, width)),
            shape((2, ROWS, EDGE, width)),
            shape((32, TILE), jnp.float32),
        ),
        in_specs=[
            SMEM,
            pl.BlockSpec((2, ROWS * SLOTS, TILE), lambda g: (g, 0, 0)),
            tile, tile, tile, tile,
            rows_spec, rows_spec, edge_spec, edge_spec, ends_spec, ends_spec,
        ],
        out_specs=(
            tile, tile, lanes(2, 8, 16), rows_spec, rows_spec, side_spec, side_spec,
            pl.BlockSpec((32, TILE), lambda g: (0, 0)),
        ),
        scratch_shapes=[
            pltpu.VMEM((ROWS, SLOTS, TILE), jnp.bfloat16),
            pltpu.VMEM((ROWS, SLOTS, TILE), jnp.bfloat16),
            pltpu.VMEM((16, 16, 2 * TILE), jnp.float32),
        ],
        cost_estimate=pl.CostEstimate(
            flops=1_500_000_000, bytes_accessed=9_000_000, transcendentals=1_000_000
        ),
        name="attend",
    )(extents, bias, queries, d_out, keys, values, top, bottom, left, right, left_ends, right_ends)

    from_left = neighbour(d_right, "col", 1)
    from_right = neighbour(d_left, "col", -1)
    piece = exchange(part.reshape(lax.axis_size("col"), -1, TILE), "col")
    from_left, from_right, piece = lax.optimization_barrier((from_left, from_right, piece))
    up, down = pl.pallas_call(
        border_body,
        out_shape=(shape(d_top.shape), shape(d_top.shape)),
        in_specs=[VMEM] * 4,
        out_specs=(VMEM, VMEM),
        name="border",
    )(d_top, d_bottom, from_left, from_right)
    up, down, piece = lax.optimization_barrier((up, down, piece))
    total = gathered(jnp.sum(gathered(jnp.sum(piece, 0), "row"), 0), "col").reshape(part.shape)
    from_below = neighbour(up, "row", -1)
    from_above = neighbour(down, "row", 1)
    d_keys, d_values, d_rel_bias = pl.pallas_call(
        final_body,
        out_shape=(shape(keys.shape), shape(keys.shape), shape(rel_bias.shape, jnp.float32)),
        in_specs=[VMEM] * 6,
        out_specs=(VMEM, VMEM, VMEM),
        name="final",
    )(own, from_left, from_right, from_above, from_below, total)
    return (attended, d_queries, d_keys, d_values, d_rel_bias)


def solution(mesh):
    tiles = P("row", "col", None)
    return jax.shard_map(
        shards,
        mesh=mesh,
        in_specs=(tiles, tiles, tiles, tiles, P(), P()),
        out_specs=(tiles, tiles, tiles, tiles, P()),
        check_vma=False,
    )
```

```python
import functools

import jax
import jax.numpy as jnp
from jax import lax
from jax.experimental import pallas as pl
from jax.experimental.pallas import tpu as pltpu
from jax.sharding import PartitionSpec as P

NEG = -1e30
HIGH = lax.Precision.HIGHEST
NT = (((1,), (1,)), ((), ()))
TN = (((0,), (0,)), ((), ()))
NN = (((1,), (0,)), ((), ()))

ROWS = 20
SLOTS = 32
OWN = 16
EDGE = 8
RAD = 6
SPAN = 13
TILE = 128
PAIRS = 6


def dot(a, b, dims, precision=None):
    return lax.dot_general(a, b, dims, precision=precision, preferred_element_type=jnp.float32)


def iota(shape, dim):
    return lax.broadcasted_iota(jnp.int32, shape, dim)


def slot_offset():
    slot = iota((SLOTS, TILE), 0)
    lane = iota((SLOTS, TILE), 1)
    column = jnp.where(
        slot < OWN, slot + RAD, jnp.where(slot < OWN + EDGE, slot - OWN - EDGE + RAD, slot - EDGE + RAD)
    )
    return column - (lane & 15), lane >> 4


def row_pick(dim):
    shape = (16, 2 * TILE)
    lane = iota(shape, 1)
    offset = ((8 - ((lane >> 4) & 7)) & 7) + 8 * (lane >> 7)
    return (iota(shape, 0) == offset).astype(jnp.float32)


def bias_body(ext_ref, table_ref, out_ref, mask_ref):
    offset, query_row = slot_offset()

    @pl.when(pl.program_id(0) == 0)
    def _():
        row, col = lax.axis_index("row"), lax.axis_index("col")
        last_row, last_col = ext_ref.shape[1] - 1, ext_ref.shape[2] - 1
        slot = iota((SLOTS, TILE), 0)
        lane = iota((SLOTS, TILE), 1)
        panel = row // 2
        valid_query = ((row % 2) * 8 + query_row < ext_ref[0, panel, col]) & (
            (lane & 15) < ext_ref[1, panel, col]
        )
        near = valid_query & (offset >= 0) & (offset < SPAN)
        local = jnp.where(slot < OWN, slot, jnp.where(slot < OWN + EDGE, slot - EDGE, slot - OWN - EDGE))
        for j in range(ROWS):
            r = row * 8 + (j - RAD + 16)
            panel_row = r // 16 - 1
            inside_row = (panel_row >= 0) & (panel_row <= last_row)
            panel_row = jnp.minimum(jnp.maximum(panel_row, 0), last_row)
            widths = []
            for step in (0, -1, 1):
                at = col + step
                inside = inside_row & (at >= 0) & (at <= last_col)
                at = jnp.minimum(jnp.maximum(at, 0), last_col)
                tall = inside & (r % 16 < ext_ref[0, panel_row, at])
                widths.append(jnp.where(tall, ext_ref[1, panel_row, at], 0))
            width = jnp.where(slot < OWN, widths[0], jnp.where(slot < OWN + EDGE, widths[1], widths[2]))
            allowed = near & (local < width) & (query_row <= j) & (query_row >= j - SPAN + 1)
            mask_ref[j * SLOTS : (j + 1) * SLOTS, :] = jnp.where(allowed, 0.0, NEG)

    spread = dot(table_ref[0], row_pick(0), NN, HIGH)
    low = jnp.zeros((SLOTS, TILE), jnp.float32)
    high = jnp.zeros((SLOTS, TILE), jnp.float32)
    for b in range(SPAN):
        low = jnp.where(offset == b, spread[b : b + 1, :TILE], low)
        high = jnp.where(offset == b, spread[b : b + 1, TILE:], high)
    for turn in range(8):
        low_turned = pltpu.roll(low, 16 * turn, 1) if turn else low
        high_turned = pltpu.roll(high, 16 * turn, 1) if turn else high
        for j in (turn, turn + 8, turn + 16):
            if j >= ROWS:
                continue
            value = low_turned if j < 8 else high_turned
            if 8 <= j < 15:
                value = jnp.where(query_row > j - 8, low_turned, high_turned)
            at = slice(j * SLOTS, (j + 1) * SLOTS)
            out_ref[0, at, :] = value + mask_ref[at, :]


def apart(x):
    first = iota((TILE, TILE), 1) < 64
    return jnp.concatenate([jnp.where(first, x, 0.0), jnp.where(first, 0.0, x)], 0)


def together(x):
    head_row = iota((TILE, TILE), 0) < 64
    return jnp.transpose(jnp.where(head_row, x[:, :TILE], x[:, TILE:]))


def attend_body(
    ext_ref, bias_ref, q_ref, g_ref, k_ref, v_ref, t_ref, b_ref, l_ref, r_ref,
    out_ref, dq_ref, own_ref, top_ref, bottom_ref, left_ref, right_ref, part_ref,
    kw_ref, vw_ref, sum_ref,
):
    for n, (own, window) in enumerate(((k_ref, kw_ref), (v_ref, vw_ref))):
        window[0:6, 0:16] = t_ref[n]
        window[6:14, 0:16] = own[...]
        window[14:20, 0:16] = b_ref[n]
        window[:, 16:24] = l_ref[n]
        window[:, 24:32] = r_ref[n]

    row, col = lax.axis_index("row"), lax.axis_index("col")
    panel = row // 2
    token = iota((TILE, TILE), 0)
    valid = ((row % 2) * 8 + (token >> 4) < ext_ref[0, panel, col]) & (
        (token & 15) < ext_ref[1, panel, col]
    )
    pairs = range(PAIRS)
    at = [slice(p * TILE, (p + 1) * TILE) for p in pairs]
    keys = [kw_ref[:, :, a].reshape(ROWS * SLOTS, TILE) for a in at]
    values = [vw_ref[:, :, a].reshape(ROWS * SLOTS, TILE) for a in at]
    queries_b = [
        apart(q_ref[:, :, a].reshape(TILE, TILE).astype(jnp.float32) * 0.125).astype(jnp.bfloat16)
        for a in at
    ]
    grads_f = [
        apart(jnp.where(valid, g_ref[:, :, a].reshape(TILE, TILE).astype(jnp.float32), 0.0)) for a in at
    ]
    grads_b = [x.astype(jnp.bfloat16) for x in grads_f]

    prob, prob_b = [], []
    for p in pairs:
        score = dot(keys[p], queries_b[p], NT)
        score = score + jnp.concatenate([bias_ref[2 * p], bias_ref[2 * p + 1]], 1)
        highest = jnp.max(score, axis=0, keepdims=True)
        weights = jnp.exp(score - highest)
        prob.append(weights * (1.0 / jnp.sum(weights, axis=0, keepdims=True)))
        prob_b.append(prob[p].astype(jnp.bfloat16))
    dscore, dscore_b = [], []
    for p in pairs:
        output = dot(values[p], prob_b[p], TN)
        delta = jnp.sum(jnp.transpose(grads_f[p]) * output, axis=0, keepdims=True)
        attended = jnp.where(valid, together(output), 0.0)
        out_ref[:, :, at[p]] = attended.astype(jnp.bfloat16).reshape(8, 16, TILE)
        dprob = dot(values[p], grads_b[p], NT)
        dscore.append(prob[p] * (dprob - delta))
        dscore_b.append(dscore[p].astype(jnp.bfloat16))

    sum_ref[...] = jnp.zeros_like(sum_ref)

    offset, query_row = slot_offset()
    for p in pairs:
        dq = together(dot(keys[p], dscore_b[p], TN)) * 0.125
        dq_ref[:, :, at[p]] = dq.astype(jnp.bfloat16).reshape(8, 16, TILE)
        dk = dot(dscore_b[p], queries_b[p], NN)
        dv = dot(prob_b[p], grads_b[p], NN)
        for n, grad in enumerate((dk, dv)):
            grad = grad.reshape(ROWS, SLOTS, TILE)
            top_ref[n, :, :, at[p]] = grad[0:6, 0:16]
            own_ref[n, :, :, at[p]] = grad[6:14, 0:16]
            bottom_ref[n, :, :, at[p]] = grad[14:20, 0:16]
            left_ref[n, :, :, at[p]] = grad[:, 16:24].astype(jnp.bfloat16)
            right_ref[n, :, :, at[p]] = grad[:, 24:32].astype(jnp.bfloat16)

        for head in range(2):
            part = dscore[p][:, head * TILE : (head + 1) * TILE]
            low = jnp.zeros((SLOTS, TILE), jnp.float32)
            high = jnp.zeros((SLOTS, TILE), jnp.float32)

            def line(j, part=part):
                return part[j * SLOTS : (j + 1) * SLOTS]

            for turn in range(8):
                x = line(turn)
                y = line(turn + 8)
                if turn < 7:
                    x = x + jnp.where(query_row > turn, y, 0.0)
                    y = jnp.where(query_row > turn, 0.0, y)
                if turn + 16 < ROWS:
                    y = y + line(turn + 16)
                back = (TILE - 16 * turn) % TILE
                low = low + (pltpu.roll(x, back, 1) if turn else x)
                high = high + (pltpu.roll(y, back, 1) if turn else y)
            index = 2 * p + head
            for b in range(SPAN):
                hit = offset == b
                sum_ref[index, b : b + 1, :TILE] = jnp.sum(
                    jnp.where(hit, low, 0.0), axis=0, keepdims=True
                )
                sum_ref[index, b : b + 1, TILE:] = jnp.sum(
                    jnp.where(hit, high, 0.0), axis=0, keepdims=True
                )

    pick = row_pick(0)
    for half in range(2):
        sums = sum_ref[half * 8 : half * 8 + 8].reshape(TILE, 2 * TILE)
        part_ref[half * 16 : half * 16 + 16, :] = dot(pick, sums, NT, HIGH)


def border_body(top_ref, bottom_ref, fl_ref, fr_ref, up_ref, down_ref):
    for source, rows, target in ((top_ref, slice(0, 6), up_ref), (bottom_ref, slice(14, 20), down_ref)):
        for n in range(2):
            low = source[n, :, :EDGE] + fl_ref[n, rows].astype(jnp.float32)
            high = source[n, :, EDGE:] + fr_ref[n, rows].astype(jnp.float32)
            target[n] = jnp.concatenate([low, high], 1).astype(jnp.bfloat16)


def final_body(own_ref, fl_ref, fr_ref, fu_ref, fd_ref, part_ref, dk_ref, dv_ref, bias_ref):
    for n, target in enumerate((dk_ref, dv_ref)):
        for r in range(8):
            left = own_ref[n, r, :EDGE] + fl_ref[n, r + RAD].astype(jnp.float32)
            right = own_ref[n, r, EDGE:] + fr_ref[n, r + RAD].astype(jnp.float32)
            total = jnp.concatenate([left, right], 0)
            if r < RAD:
                total = total + fu_ref[n, r].astype(jnp.float32)
            if r >= 8 - RAD:
                total = total + fd_ref[n, r - 8 + RAD].astype(jnp.float32)
            target[r] = total.astype(jnp.bfloat16)
    for h in range(bias_ref.shape[0]):
        at = (h % 8) * 16
        bias_ref[h] = part_ref[(h // 8) * 16 : (h // 8) * 16 + SPAN, at : at + SPAN]


def neighbour(value, axis, step):
    size = lax.axis_size(axis)
    return lax.ppermute(value, axis, [(i, i + step) for i in range(size) if 0 <= i + step < size])


def exchange(value, axis):
    return lax.all_to_all(value, axis, 0, 0)


def gathered(piece, axis):
    return exchange(jnp.broadcast_to(piece, (lax.axis_size(axis),) + piece.shape), axis)


def shape(dims, dtype=jnp.bfloat16):
    return jax.ShapeDtypeStruct(dims, dtype)


LIMIT = 32 << 20
SMEM = pl.BlockSpec(memory_space=pltpu.SMEM)
VMEM = pl.BlockSpec(memory_space=pltpu.VMEM)


def shards(queries, keys, values, d_out, extents, rel_bias):
    heads = rel_bias.shape[0]
    width = queries.shape[2]
    both = jnp.stack([keys, values])
    top = neighbour(both[:, 2:], "row", 1)
    bottom = neighbour(both[:, :6], "row", -1)

    table = jnp.pad(jnp.swapaxes(rel_bias, 1, 2), ((0, 0), (0, 3), (0, 3)))
    bias = pl.pallas_call(
        bias_body,
        grid=(heads,),
        out_shape=shape((heads, ROWS * SLOTS, TILE), jnp.float32),
        in_specs=[SMEM, pl.BlockSpec((1, 16, 16), lambda h: (h, 0, 0))],
        out_specs=pl.BlockSpec((1, ROWS * SLOTS, TILE), lambda h: (h, 0, 0)),
        scratch_shapes=[pltpu.VMEM((ROWS * SLOTS, TILE), jnp.float32)],
        cost_estimate=pl.CostEstimate(flops=20_000_000, bytes_accessed=4_000_000, transcendentals=0),
        compiler_params=pltpu.CompilerParams(vmem_limit_bytes=LIMIT),
        name="bias_mask",
    )(extents, table)

    top, bottom, bias = lax.optimization_barrier((top, bottom, bias))
    band = jnp.concatenate([top, both, bottom], 1)
    left = neighbour(band[:, :, EDGE:], "col", 1)
    right = neighbour(band[:, :, :EDGE], "col", -1)

    attended, d_queries, own, d_top, d_bottom, d_left, d_right, part = pl.pallas_call(
        attend_body,
        out_shape=(
            shape(queries.shape),
            shape(queries.shape),
            shape((2, 8, 16, width), jnp.float32),
            shape((2, 6, 16, width), jnp.float32),
            shape((2, 6, 16, width), jnp.float32),
            shape((2, ROWS, EDGE, width)),
            shape((2, ROWS, EDGE, width)),
            shape((32, TILE), jnp.float32),
        ),
        in_specs=[SMEM] + [VMEM] * 9,
        out_specs=(VMEM,) * 8,
        scratch_shapes=[
            pltpu.VMEM((ROWS, SLOTS, PAIRS * TILE), jnp.bfloat16),
            pltpu.VMEM((ROWS, SLOTS, PAIRS * TILE), jnp.bfloat16),
            pltpu.VMEM((16, 16, 2 * TILE), jnp.float32),
        ],
        cost_estimate=pl.CostEstimate(
            flops=1_500_000_000, bytes_accessed=9_000_000, transcendentals=1_000_000
        ),
        compiler_params=pltpu.CompilerParams(vmem_limit_bytes=LIMIT),
        name="attend",
    )(extents, bias, queries, d_out, keys, values, top, bottom, left, right)

    piece = exchange(part.reshape(lax.axis_size("col"), -1, TILE), "col")
    d_left, d_right, piece = lax.optimization_barrier((d_left, d_right, piece))
    from_left = neighbour(d_right, "col", 1)
    from_right = neighbour(d_left, "col", -1)
    piece = gathered(jnp.sum(piece, 0), "row")
    from_left, from_right, piece = lax.optimization_barrier((from_left, from_right, piece))
    up, down = pl.pallas_call(
        border_body,
        out_shape=(shape(d_top.shape), shape(d_top.shape)),
        in_specs=[VMEM] * 4,
        out_specs=(VMEM, VMEM),
        compiler_params=pltpu.CompilerParams(vmem_limit_bytes=LIMIT),
        name="border",
    )(d_top, d_bottom, from_left, from_right)
    up, down, piece = lax.optimization_barrier((up, down, piece))
    total = gathered(jnp.sum(piece, 0), "col").reshape(part.shape)
    from_below = neighbour(up, "row", -1)
    from_above = neighbour(down, "row", 1)
    d_keys, d_values, d_rel_bias = pl.pallas_call(
        final_body,
        out_shape=(shape(keys.shape), shape(keys.shape), shape(rel_bias.shape, jnp.float32)),
        in_specs=[VMEM] * 6,
        out_specs=(VMEM, VMEM, VMEM),
        compiler_params=pltpu.CompilerParams(vmem_limit_bytes=LIMIT),
        name="final",
    )(own, from_left, from_right, from_above, from_below, total)
    return (attended, d_queries, d_keys, d_values, d_rel_bias)


def solution(mesh):
    tiles = P("row", "col", None)
    return jax.shard_map(
        shards,
        mesh=mesh,
        in_specs=(tiles, tiles, tiles, tiles, P(), P()),
        out_specs=(tiles, tiles, tiles, tiles, P()),
        check_vma=False,
    )
```

```python
import functools

import jax
import jax.numpy as jnp
from jax import lax
from jax.experimental import pallas as pl
from jax.experimental.pallas import tpu as pltpu
from jax.sharding import PartitionSpec as P

NEG = -1e30
HIGH = lax.Precision.HIGHEST
NT = (((1,), (1,)), ((), ()))
TN = (((0,), (0,)), ((), ()))
NN = (((1,), (0,)), ((), ()))

ROWS = 20
SLOTS = 32
OWN = 16
EDGE = 8
RAD = 6
SPAN = 13
TILE = 128
PAIRS = 6


def dot(a, b, dims, precision=None):
    return lax.dot_general(a, b, dims, precision=precision, preferred_element_type=jnp.float32)


def iota(shape, dim):
    return lax.broadcasted_iota(jnp.int32, shape, dim)


def slot_offset():
    slot = iota((SLOTS, TILE), 0)
    lane = iota((SLOTS, TILE), 1)
    column = jnp.where(
        slot < OWN, slot + RAD, jnp.where(slot < OWN + EDGE, slot - OWN - EDGE + RAD, slot - EDGE + RAD)
    )
    return column - (lane & 15), lane >> 4


def row_pick(dim):
    shape = (16, 2 * TILE)
    lane = iota(shape, 1)
    offset = ((8 - ((lane >> 4) & 7)) & 7) + 8 * (lane >> 7)
    return (iota(shape, 0) == offset).astype(jnp.float32)


def bias_body(ext_ref, table_ref, out_ref, mask_ref):
    offset, query_row = slot_offset()

    @pl.when(pl.program_id(0) == 0)
    def _():
        row, col = lax.axis_index("row"), lax.axis_index("col")
        last_row, last_col = ext_ref.shape[1] - 1, ext_ref.shape[2] - 1
        slot = iota((SLOTS, TILE), 0)
        lane = iota((SLOTS, TILE), 1)
        panel = row // 2
        valid_query = ((row % 2) * 8 + query_row < ext_ref[0, panel, col]) & (
            (lane & 15) < ext_ref[1, panel, col]
        )
        near = valid_query & (offset >= 0) & (offset < SPAN)
        local = jnp.where(slot < OWN, slot, jnp.where(slot < OWN + EDGE, slot - EDGE, slot - OWN - EDGE))
        for j in range(ROWS):
            r = row * 8 + (j - RAD + 16)
            panel_row = r // 16 - 1
            inside_row = (panel_row >= 0) & (panel_row <= last_row)
            panel_row = jnp.minimum(jnp.maximum(panel_row, 0), last_row)
            widths = []
            for step in (0, -1, 1):
                at = col + step
                inside = inside_row & (at >= 0) & (at <= last_col)
                at = jnp.minimum(jnp.maximum(at, 0), last_col)
                tall = inside & (r % 16 < ext_ref[0, panel_row, at])
                widths.append(jnp.where(tall, ext_ref[1, panel_row, at], 0))
            width = jnp.where(slot < OWN, widths[0], jnp.where(slot < OWN + EDGE, widths[1], widths[2]))
            allowed = near & (local < width) & (query_row <= j) & (query_row >= j - SPAN + 1)
            mask_ref[j * SLOTS : (j + 1) * SLOTS, :] = jnp.where(allowed, 0.0, NEG)

    spread = dot(table_ref[0], row_pick(0), NN, HIGH)
    low = jnp.zeros((SLOTS, TILE), jnp.float32)
    high = jnp.zeros((SLOTS, TILE), jnp.float32)
    for b in range(SPAN):
        low = jnp.where(offset == b, spread[b : b + 1, :TILE], low)
        high = jnp.where(offset == b, spread[b : b + 1, TILE:], high)
    for turn in range(8):
        low_turned = pltpu.roll(low, 16 * turn, 1) if turn else low
        high_turned = pltpu.roll(high, 16 * turn, 1) if turn else high
        for j in (turn, turn + 8, turn + 16):
            if j >= ROWS:
                continue
            value = low_turned if j < 8 else high_turned
            if 8 <= j < 15:
                value = jnp.where(query_row > j - 8, low_turned, high_turned)
            at = slice(j * SLOTS, (j + 1) * SLOTS)
            out_ref[0, at, :] = value + mask_ref[at, :]


def apart(x):
    first = iota((TILE, TILE), 1) < 64
    return jnp.concatenate([jnp.where(first, x, 0.0), jnp.where(first, 0.0, x)], 0)


def together(x):
    head_row = iota((TILE, TILE), 0) < 64
    return jnp.transpose(jnp.where(head_row, x[:, :TILE], x[:, TILE:]))


def attend_body(
    ext_ref, bias_ref, q_ref, g_ref, k_ref, v_ref, t_ref, b_ref, near_ref, far_ref,
    out_ref, dq_ref, own_ref, top_ref, bottom_ref, left_ref, right_ref, part_ref,
    kw_ref, vw_ref, sum_ref,
):
    for n, (own, window) in enumerate(((k_ref, kw_ref), (v_ref, vw_ref))):
        window[0:6, 0:16] = t_ref[n]
        window[6:14, 0:16] = own[...]
        window[14:20, 0:16] = b_ref[n]

    row, col = lax.axis_index("row"), lax.axis_index("col")
    for parity, l_ref, r_ref in ((0, far_ref, near_ref), (1, near_ref, far_ref)):

        @pl.when(col % 2 == parity)
        def _(l_ref=l_ref, r_ref=r_ref):
            for n, window in enumerate((kw_ref, vw_ref)):
                window[:, 16:24] = l_ref[n]
                window[:, 24:32] = r_ref[n]

    panel = row // 2
    token = iota((TILE, TILE), 0)
    valid = ((row % 2) * 8 + (token >> 4) < ext_ref[0, panel, col]) & (
        (token & 15) < ext_ref[1, panel, col]
    )
    pairs = range(PAIRS)
    at = [slice(p * TILE, (p + 1) * TILE) for p in pairs]
    keys = [kw_ref[:, :, a].reshape(ROWS * SLOTS, TILE) for a in at]
    values = [vw_ref[:, :, a].reshape(ROWS * SLOTS, TILE) for a in at]
    queries_b = [
        apart(q_ref[:, :, a].reshape(TILE, TILE).astype(jnp.float32) * 0.125).astype(jnp.bfloat16)
        for a in at
    ]
    grads_f = [
        apart(jnp.where(valid, g_ref[:, :, a].reshape(TILE, TILE).astype(jnp.float32), 0.0)) for a in at
    ]
    grads_b = [x.astype(jnp.bfloat16) for x in grads_f]

    prob, prob_b = [], []
    for p in pairs:
        score = dot(keys[p], queries_b[p], NT)
        score = score + jnp.concatenate([bias_ref[2 * p], bias_ref[2 * p + 1]], 1)
        highest = jnp.max(score, axis=0, keepdims=True)
        weights = jnp.exp(score - highest)
        prob.append(weights * (1.0 / jnp.sum(weights, axis=0, keepdims=True)))
        prob_b.append(prob[p].astype(jnp.bfloat16))
    dscore, dscore_b = [], []
    for p in pairs:
        output = dot(values[p], prob_b[p], TN)
        delta = jnp.sum(jnp.transpose(grads_f[p]) * output, axis=0, keepdims=True)
        attended = jnp.where(valid, together(output), 0.0)
        out_ref[:, :, at[p]] = attended.astype(jnp.bfloat16).reshape(8, 16, TILE)
        dprob = dot(values[p], grads_b[p], NT)
        dscore.append(prob[p] * (dprob - delta))
        dscore_b.append(dscore[p].astype(jnp.bfloat16))

    sum_ref[...] = jnp.zeros_like(sum_ref)

    offset, query_row = slot_offset()
    for p in pairs:
        dq = together(dot(keys[p], dscore_b[p], TN)) * 0.125
        dq_ref[:, :, at[p]] = dq.astype(jnp.bfloat16).reshape(8, 16, TILE)
        dk = dot(dscore_b[p], queries_b[p], NN)
        dv = dot(prob_b[p], grads_b[p], NN)
        for n, grad in enumerate((dk, dv)):
            grad = grad.reshape(ROWS, SLOTS, TILE)
            top_ref[n, :, :, at[p]] = grad[0:6, 0:16]
            own_ref[n, :, :, at[p]] = grad[6:14, 0:16]
            bottom_ref[n, :, :, at[p]] = grad[14:20, 0:16]
            left_ref[n, :, :, at[p]] = grad[:, 16:24].astype(jnp.bfloat16)
            right_ref[n, :, :, at[p]] = grad[:, 24:32].astype(jnp.bfloat16)

        for head in range(2):
            part = dscore[p][:, head * TILE : (head + 1) * TILE]
            low = jnp.zeros((SLOTS, TILE), jnp.float32)
            high = jnp.zeros((SLOTS, TILE), jnp.float32)

            def line(j, part=part):
                return part[j * SLOTS : (j + 1) * SLOTS]

            for turn in range(8):
                x = line(turn)
                y = line(turn + 8)
                if turn < 7:
                    x = x + jnp.where(query_row > turn, y, 0.0)
                    y = jnp.where(query_row > turn, 0.0, y)
                if turn + 16 < ROWS:
                    y = y + line(turn + 16)
                back = (TILE - 16 * turn) % TILE
                low = low + (pltpu.roll(x, back, 1) if turn else x)
                high = high + (pltpu.roll(y, back, 1) if turn else y)
            index = 2 * p + head
            for b in range(SPAN):
                hit = offset == b
                sum_ref[index, b : b + 1, :TILE] = jnp.sum(
                    jnp.where(hit, low, 0.0), axis=0, keepdims=True
                )
                sum_ref[index, b : b + 1, TILE:] = jnp.sum(
                    jnp.where(hit, high, 0.0), axis=0, keepdims=True
                )

    pick = row_pick(0)
    for half in range(2):
        sums = sum_ref[half * 8 : half * 8 + 8].reshape(TILE, 2 * TILE)
        part_ref[half * 16 : half * 16 + 16, :] = dot(pick, sums, NT, HIGH)


def sides(near, far):
    near, far = near.astype(jnp.float32), far.astype(jnp.float32)
    even = lax.axis_index("col") % 2 == 0
    return jnp.where(even, far, near), jnp.where(even, near, far)


def border_body(top_ref, bottom_ref, near_ref, far_ref, up_ref, down_ref):
    for source, rows, target in ((top_ref, slice(0, 6), up_ref), (bottom_ref, slice(14, 20), down_ref)):
        for n in range(2):
            left, right = sides(near_ref[n, rows], far_ref[n, rows])
            low = source[n, :, :EDGE] + left
            high = source[n, :, EDGE:] + right
            target[n] = jnp.concatenate([low, high], 1).astype(jnp.bfloat16)


def final_body(own_ref, near_ref, far_ref, fu_ref, fd_ref, part_ref, dk_ref, dv_ref, bias_ref):
    for n, target in enumerate((dk_ref, dv_ref)):
        for r in range(8):
            left, right = sides(near_ref[n, r + RAD], far_ref[n, r + RAD])
            total = jnp.concatenate([own_ref[n, r, :EDGE] + left, own_ref[n, r, EDGE:] + right], 0)
            if r < RAD:
                total = total + fu_ref[n, r].astype(jnp.float32)
            if r >= 8 - RAD:
                total = total + fd_ref[n, r - 8 + RAD].astype(jnp.float32)
            target[r] = total.astype(jnp.bfloat16)
    for h in range(bias_ref.shape[0]):
        at = (h % 8) * 16
        bias_ref[h] = part_ref[(h // 8) * 16 : (h // 8) * 16 + SPAN, at : at + SPAN]


def neighbour(value, axis, step):
    size = lax.axis_size(axis)
    return lax.ppermute(value, axis, [(i, i + step) for i in range(size) if 0 <= i + step < size])


def swap(value, axis, first):
    pairs = [(i, i + 1) for i in range(first, lax.axis_size(axis) - 1, 2)]
    return lax.ppermute(value, axis, pairs + [(j, i) for i, j in pairs])


def exchange(value, axis):
    return lax.all_to_all(value, axis, 0, 0)


def gathered(piece, axis):
    return exchange(jnp.broadcast_to(piece, (lax.axis_size(axis),) + piece.shape), axis)


def shape(dims, dtype=jnp.bfloat16):
    return jax.ShapeDtypeStruct(dims, dtype)


LIMIT = 32 << 20
SMEM = pl.BlockSpec(memory_space=pltpu.SMEM)
VMEM = pl.BlockSpec(memory_space=pltpu.VMEM)


def shards(queries, keys, values, d_out, extents, rel_bias):
    heads = rel_bias.shape[0]
    width = queries.shape[2]
    both = jnp.stack([keys, values])
    top = neighbour(both[:, 2:], "row", 1)
    bottom = neighbour(both[:, :6], "row", -1)

    table = jnp.pad(jnp.swapaxes(rel_bias, 1, 2), ((0, 0), (0, 3), (0, 3)))
    bias = pl.pallas_call(
        bias_body,
        grid=(heads,),
        out_shape=shape((heads, ROWS * SLOTS, TILE), jnp.float32),
        in_specs=[SMEM, pl.BlockSpec((1, 16, 16), lambda h: (h, 0, 0))],
        out_specs=pl.BlockSpec((1, ROWS * SLOTS, TILE), lambda h: (h, 0, 0)),
        scratch_shapes=[pltpu.VMEM((ROWS * SLOTS, TILE), jnp.float32)],
        cost_estimate=pl.CostEstimate(flops=20_000_000, bytes_accessed=4_000_000, transcendentals=0),
        compiler_params=pltpu.CompilerParams(vmem_limit_bytes=LIMIT),
        name="bias_mask",
    )(extents, table)

    top, bottom, bias = lax.optimization_barrier((top, bottom, bias))
    band = jnp.concatenate([top, both, bottom], 1)
    even = lax.axis_index("col") % 2 == 0
    low, high = band[:, :, :EDGE], band[:, :, EDGE:]
    near = swap(jnp.where(even, high, low), "col", 0)
    far = swap(jnp.where(even, low, high), "col", 1)

    attended, d_queries, own, d_top, d_bottom, d_left, d_right, part = pl.pallas_call(
        attend_body,
        out_shape=(
            shape(queries.shape),
            shape(queries.shape),
            shape((2, 8, 16, width), jnp.float32),
            shape((2, 6, 16, width), jnp.float32),
            shape((2, 6, 16, width), jnp.float32),
            shape((2, ROWS, EDGE, width)),
            shape((2, ROWS, EDGE, width)),
            shape((32, TILE), jnp.float32),
        ),
        in_specs=[SMEM] + [VMEM] * 9,
        out_specs=(VMEM,) * 8,
        scratch_shapes=[
            pltpu.VMEM((ROWS, SLOTS, PAIRS * TILE), jnp.bfloat16),
            pltpu.VMEM((ROWS, SLOTS, PAIRS * TILE), jnp.bfloat16),
            pltpu.VMEM((16, 16, 2 * TILE), jnp.float32),
        ],
        cost_estimate=pl.CostEstimate(
            flops=1_500_000_000, bytes_accessed=9_000_000, transcendentals=1_000_000
        ),
        compiler_params=pltpu.CompilerParams(vmem_limit_bytes=LIMIT),
        name="attend",
    )(extents, bias, queries, d_out, keys, values, top, bottom, near, far)

    piece = exchange(part.reshape(lax.axis_size("col"), -1, TILE), "col")
    d_left, d_right, piece = lax.optimization_barrier((d_left, d_right, piece))
    from_near = swap(jnp.where(even, d_right, d_left), "col", 0)
    from_far = swap(jnp.where(even, d_left, d_right), "col", 1)
    piece = gathered(jnp.sum(piece, 0), "row")
    from_near, from_far, piece = lax.optimization_barrier((from_near, from_far, piece))
    up, down = pl.pallas_call(
        border_body,
        out_shape=(shape(d_top.shape), shape(d_top.shape)),
        in_specs=[VMEM] * 4,
        out_specs=(VMEM, VMEM),
        compiler_params=pltpu.CompilerParams(vmem_limit_bytes=LIMIT),
        name="border",
    )(d_top, d_bottom, from_near, from_far)
    up, down, piece = lax.optimization_barrier((up, down, piece))
    total = gathered(jnp.sum(piece, 0), "col").reshape(part.shape)
    from_below = neighbour(up, "row", -1)
    from_above = neighbour(down, "row", 1)
    d_keys, d_values, d_rel_bias = pl.pallas_call(
        final_body,
        out_shape=(shape(keys.shape), shape(keys.shape), shape(rel_bias.shape, jnp.float32)),
        in_specs=[VMEM] * 6,
        out_specs=(VMEM, VMEM, VMEM),
        compiler_params=pltpu.CompilerParams(vmem_limit_bytes=LIMIT),
        name="final",
    )(own, from_near, from_far, from_above, from_below, total)
    return (attended, d_queries, d_keys, d_values, d_rel_bias)


def solution(mesh):
    tiles = P("row", "col", None)
    return jax.shard_map(
        shards,
        mesh=mesh,
        in_specs=(tiles, tiles, tiles, tiles, P(), P()),
        out_specs=(tiles, tiles, tiles, tiles, P()),
        check_vma=False,
    )
```

```python
import functools

import jax
import jax.numpy as jnp
from jax import lax
from jax.experimental import pallas as pl
from jax.experimental.pallas import tpu as pltpu
from jax.sharding import PartitionSpec as P

NEG = -1e30
HIGH = lax.Precision.HIGHEST
NT = (((1,), (1,)), ((), ()))
TN = (((0,), (0,)), ((), ()))
NN = (((1,), (0,)), ((), ()))

ROWS = 20
SLOTS = 32
OWN = 16
EDGE = 8
RAD = 6
SPAN = 13
TILE = 128
PAIRS = 6


def dot(a, b, dims, precision=None):
    return lax.dot_general(a, b, dims, precision=precision, preferred_element_type=jnp.float32)


def iota(shape, dim):
    return lax.broadcasted_iota(jnp.int32, shape, dim)


def slot_offset():
    slot = iota((SLOTS, TILE), 0)
    lane = iota((SLOTS, TILE), 1)
    column = jnp.where(
        slot < OWN, slot + RAD, jnp.where(slot < OWN + EDGE, slot - OWN - EDGE + RAD, slot - EDGE + RAD)
    )
    return column - (lane & 15), lane >> 4


def row_pick(dim):
    shape = (16, 2 * TILE)
    lane = iota(shape, 1)
    offset = ((8 - ((lane >> 4) & 7)) & 7) + 8 * (lane >> 7)
    return (iota(shape, 0) == offset).astype(jnp.float32)


def bias_body(ext_ref, table_ref, out_ref, mask_ref):
    offset, query_row = slot_offset()

    @pl.when(pl.program_id(0) == 0)
    def _():
        row, col = lax.axis_index("row"), lax.axis_index("col")
        last_row, last_col = ext_ref.shape[1] - 1, ext_ref.shape[2] - 1
        slot = iota((SLOTS, TILE), 0)
        lane = iota((SLOTS, TILE), 1)
        panel = row // 2
        valid_query = ((row % 2) * 8 + query_row < ext_ref[0, panel, col]) & (
            (lane & 15) < ext_ref[1, panel, col]
        )
        near = valid_query & (offset >= 0) & (offset < SPAN)
        local = jnp.where(slot < OWN, slot, jnp.where(slot < OWN + EDGE, slot - EDGE, slot - OWN - EDGE))
        for j in range(ROWS):
            r = row * 8 + (j - RAD + 16)
            panel_row = r // 16 - 1
            inside_row = (panel_row >= 0) & (panel_row <= last_row)
            panel_row = jnp.minimum(jnp.maximum(panel_row, 0), last_row)
            widths = []
            for step in (0, -1, 1):
                at = col + step
                inside = inside_row & (at >= 0) & (at <= last_col)
                at = jnp.minimum(jnp.maximum(at, 0), last_col)
                tall = inside & (r % 16 < ext_ref[0, panel_row, at])
                widths.append(jnp.where(tall, ext_ref[1, panel_row, at], 0))
            width = jnp.where(slot < OWN, widths[0], jnp.where(slot < OWN + EDGE, widths[1], widths[2]))
            allowed = near & (local < width) & (query_row <= j) & (query_row >= j - SPAN + 1)
            mask_ref[j * SLOTS : (j + 1) * SLOTS, :] = jnp.where(allowed, 0.0, NEG)

    spread = dot(table_ref[0], row_pick(0), NN, HIGH)
    low = jnp.zeros((SLOTS, TILE), jnp.float32)
    high = jnp.zeros((SLOTS, TILE), jnp.float32)
    for b in range(SPAN):
        low = jnp.where(offset == b, spread[b : b + 1, :TILE], low)
        high = jnp.where(offset == b, spread[b : b + 1, TILE:], high)
    for turn in range(8):
        low_turned = pltpu.roll(low, 16 * turn, 1) if turn else low
        high_turned = pltpu.roll(high, 16 * turn, 1) if turn else high
        for j in (turn, turn + 8, turn + 16):
            if j >= ROWS:
                continue
            value = low_turned if j < 8 else high_turned
            if 8 <= j < 15:
                value = jnp.where(query_row > j - 8, low_turned, high_turned)
            at = slice(j * SLOTS, (j + 1) * SLOTS)
            out_ref[0, at, :] = value + mask_ref[at, :]


def apart(x):
    first = iota((TILE, TILE), 1) < 64
    return jnp.concatenate([jnp.where(first, x, 0.0), jnp.where(first, 0.0, x)], 0)


def together(x):
    head_row = iota((TILE, TILE), 0) < 64
    return jnp.transpose(jnp.where(head_row, x[:, :TILE], x[:, TILE:]))


def attend_body(
    ext_ref, bias_ref, q_ref, g_ref, k_ref, v_ref, near_row_ref, far_row_ref, near_ref, far_ref,
    out_ref, dq_ref, own_ref, top_ref, bottom_ref, left_ref, right_ref, part_ref,
    kw_ref, vw_ref, sum_ref,
):
    for n, (own, window) in enumerate(((k_ref, kw_ref), (v_ref, vw_ref))):
        window[6:14, 0:16] = own[...]

    row, col = lax.axis_index("row"), lax.axis_index("col")
    for parity, l_ref, r_ref in ((0, far_ref, near_ref), (1, near_ref, far_ref)):

        @pl.when(col % 2 == parity)
        def _(l_ref=l_ref, r_ref=r_ref):
            for n, window in enumerate((kw_ref, vw_ref)):
                window[:, 16:24] = l_ref[n]
                window[:, 24:32] = r_ref[n]

    for parity, t_ref, b_ref in ((0, far_row_ref, near_row_ref), (1, near_row_ref, far_row_ref)):

        @pl.when(row % 2 == parity)
        def _(t_ref=t_ref, b_ref=b_ref):
            for n, window in enumerate((kw_ref, vw_ref)):
                window[0:6, 0:16] = t_ref[n]
                window[14:20, 0:16] = b_ref[n]

    panel = row // 2
    token = iota((TILE, TILE), 0)
    valid = ((row % 2) * 8 + (token >> 4) < ext_ref[0, panel, col]) & (
        (token & 15) < ext_ref[1, panel, col]
    )
    pairs = range(PAIRS)
    at = [slice(p * TILE, (p + 1) * TILE) for p in pairs]
    keys = [kw_ref[:, :, a].reshape(ROWS * SLOTS, TILE) for a in at]
    values = [vw_ref[:, :, a].reshape(ROWS * SLOTS, TILE) for a in at]
    queries_b = [
        apart(q_ref[:, :, a].reshape(TILE, TILE).astype(jnp.float32) * 0.125).astype(jnp.bfloat16)
        for a in at
    ]
    grads_f = [
        apart(jnp.where(valid, g_ref[:, :, a].reshape(TILE, TILE).astype(jnp.float32), 0.0)) for a in at
    ]
    grads_b = [x.astype(jnp.bfloat16) for x in grads_f]

    prob, prob_b = [], []
    for p in pairs:
        score = dot(keys[p], queries_b[p], NT)
        score = score + jnp.concatenate([bias_ref[2 * p], bias_ref[2 * p + 1]], 1)
        highest = jnp.max(score, axis=0, keepdims=True)
        weights = jnp.exp(score - highest)
        prob.append(weights * (1.0 / jnp.sum(weights, axis=0, keepdims=True)))
        prob_b.append(prob[p].astype(jnp.bfloat16))
    dscore, dscore_b = [], []
    for p in pairs:
        output = dot(values[p], prob_b[p], TN)
        delta = jnp.sum(jnp.transpose(grads_f[p]) * output, axis=0, keepdims=True)
        attended = jnp.where(valid, together(output), 0.0)
        out_ref[:, :, at[p]] = attended.astype(jnp.bfloat16).reshape(8, 16, TILE)
        dprob = dot(values[p], grads_b[p], NT)
        dscore.append(prob[p] * (dprob - delta))
        dscore_b.append(dscore[p].astype(jnp.bfloat16))

    sum_ref[...] = jnp.zeros_like(sum_ref)

    offset, query_row = slot_offset()
    for p in pairs:
        dq = together(dot(keys[p], dscore_b[p], TN)) * 0.125
        dq_ref[:, :, at[p]] = dq.astype(jnp.bfloat16).reshape(8, 16, TILE)
        dk = dot(dscore_b[p], queries_b[p], NN)
        dv = dot(prob_b[p], grads_b[p], NN)
        for n, grad in enumerate((dk, dv)):
            grad = grad.reshape(ROWS, SLOTS, TILE)
            top_ref[n, :, :, at[p]] = grad[0:6, 0:16]
            own_ref[n, :, :, at[p]] = grad[6:14, 0:16]
            bottom_ref[n, :, :, at[p]] = grad[14:20, 0:16]
            left_ref[n, :, :, at[p]] = grad[:, 16:24].astype(jnp.bfloat16)
            right_ref[n, :, :, at[p]] = grad[:, 24:32].astype(jnp.bfloat16)

        for head in range(2):
            part = dscore[p][:, head * TILE : (head + 1) * TILE]
            low = jnp.zeros((SLOTS, TILE), jnp.float32)
            high = jnp.zeros((SLOTS, TILE), jnp.float32)

            def line(j, part=part):
                return part[j * SLOTS : (j + 1) * SLOTS]

            for turn in range(8):
                x = line(turn)
                y = line(turn + 8)
                if turn < 7:
                    x = x + jnp.where(query_row > turn, y, 0.0)
                    y = jnp.where(query_row > turn, 0.0, y)
                if turn + 16 < ROWS:
                    y = y + line(turn + 16)
                back = (TILE - 16 * turn) % TILE
                low = low + (pltpu.roll(x, back, 1) if turn else x)
                high = high + (pltpu.roll(y, back, 1) if turn else y)
            index = 2 * p + head
            for b in range(SPAN):
                hit = offset == b
                sum_ref[index, b : b + 1, :TILE] = jnp.sum(
                    jnp.where(hit, low, 0.0), axis=0, keepdims=True
                )
                sum_ref[index, b : b + 1, TILE:] = jnp.sum(
                    jnp.where(hit, high, 0.0), axis=0, keepdims=True
                )

    pick = row_pick(0)
    for half in range(2):
        sums = sum_ref[half * 8 : half * 8 + 8].reshape(TILE, 2 * TILE)
        part_ref[half * 16 : half * 16 + 16, :] = dot(pick, sums, NT, HIGH)


def sides(near, far, axis="col"):
    near, far = near.astype(jnp.float32), far.astype(jnp.float32)
    even = lax.axis_index(axis) % 2 == 0
    return jnp.where(even, far, near), jnp.where(even, near, far)


def border_body(top_ref, bottom_ref, near_ref, far_ref, near_out_ref, far_out_ref):
    even = lax.axis_index("row") % 2 == 0
    for n in range(2):
        up, down = [], []
        for source, rows, target in ((top_ref, slice(0, 6), up), (bottom_ref, slice(14, 20), down)):
            left, right = sides(near_ref[n, rows], far_ref[n, rows])
            target.append(
                jnp.concatenate([source[n, :, :EDGE] + left, source[n, :, EDGE:] + right], 1)
            )
        near_out_ref[n] = jnp.where(even, down[0], up[0]).astype(jnp.bfloat16)
        far_out_ref[n] = jnp.where(even, up[0], down[0]).astype(jnp.bfloat16)


def final_body(own_ref, near_ref, far_ref, near_row_ref, far_row_ref, part_ref, dk_ref, dv_ref, bias_ref):
    for n, target in enumerate((dk_ref, dv_ref)):
        above, below = sides(near_row_ref[n], far_row_ref[n], "row")
        for r in range(8):
            left, right = sides(near_ref[n, r + RAD], far_ref[n, r + RAD])
            total = jnp.concatenate([own_ref[n, r, :EDGE] + left, own_ref[n, r, EDGE:] + right], 0)
            if r < RAD:
                total = total + above[r]
            if r >= 8 - RAD:
                total = total + below[r - 8 + RAD]
            target[r] = total.astype(jnp.bfloat16)
    for h in range(bias_ref.shape[0]):
        at = (h % 8) * 16
        bias_ref[h] = part_ref[(h // 8) * 16 : (h // 8) * 16 + SPAN, at : at + SPAN]


def swap(value, axis, first):
    pairs = [(i, i + 1) for i in range(first, lax.axis_size(axis) - 1, 2)]
    return lax.ppermute(value, axis, pairs + [(j, i) for i, j in pairs])


def exchange(value, axis):
    return lax.all_to_all(value, axis, 0, 0)


def gathered(piece, axis):
    return exchange(jnp.broadcast_to(piece, (lax.axis_size(axis),) + piece.shape), axis)


def shape(dims, dtype=jnp.bfloat16):
    return jax.ShapeDtypeStruct(dims, dtype)


LIMIT = 32 << 20
SMEM = pl.BlockSpec(memory_space=pltpu.SMEM)
VMEM = pl.BlockSpec(memory_space=pltpu.VMEM)


def shards(queries, keys, values, d_out, extents, rel_bias):
    heads = rel_bias.shape[0]
    width = queries.shape[2]
    both = jnp.stack([keys, values])
    even_row = lax.axis_index("row") % 2 == 0
    upper, lower = both[:, :6], both[:, 2:]
    near_row = swap(jnp.where(even_row, lower, upper), "row", 0)
    far_row = swap(jnp.where(even_row, upper, lower), "row", 1)

    table = jnp.pad(jnp.swapaxes(rel_bias, 1, 2), ((0, 0), (0, 3), (0, 3)))
    bias = pl.pallas_call(
        bias_body,
        grid=(heads,),
        out_shape=shape((heads, ROWS * SLOTS, TILE), jnp.float32),
        in_specs=[SMEM, pl.BlockSpec((1, 16, 16), lambda h: (h, 0, 0))],
        out_specs=pl.BlockSpec((1, ROWS * SLOTS, TILE), lambda h: (h, 0, 0)),
        scratch_shapes=[pltpu.VMEM((ROWS * SLOTS, TILE), jnp.float32)],
        cost_estimate=pl.CostEstimate(flops=20_000_000, bytes_accessed=4_000_000, transcendentals=0),
        compiler_params=pltpu.CompilerParams(vmem_limit_bytes=LIMIT),
        name="bias_mask",
    )(extents, table)

    near_row, far_row, bias = lax.optimization_barrier((near_row, far_row, bias))
    top, bottom = jnp.where(even_row, far_row, near_row), jnp.where(even_row, near_row, far_row)
    band = jnp.concatenate([top, both, bottom], 1)
    even = lax.axis_index("col") % 2 == 0
    low, high = band[:, :, :EDGE], band[:, :, EDGE:]
    near = swap(jnp.where(even, high, low), "col", 0)
    far = swap(jnp.where(even, low, high), "col", 1)

    attended, d_queries, own, d_top, d_bottom, d_left, d_right, part = pl.pallas_call(
        attend_body,
        out_shape=(
            shape(queries.shape),
            shape(queries.shape),
            shape((2, 8, 16, width), jnp.float32),
            shape((2, 6, 16, width), jnp.float32),
            shape((2, 6, 16, width), jnp.float32),
            shape((2, ROWS, EDGE, width)),
            shape((2, ROWS, EDGE, width)),
            shape((32, TILE), jnp.float32),
        ),
        in_specs=[SMEM] + [VMEM] * 9,
        out_specs=(VMEM,) * 8,
        scratch_shapes=[
            pltpu.VMEM((ROWS, SLOTS, PAIRS * TILE), jnp.bfloat16),
            pltpu.VMEM((ROWS, SLOTS, PAIRS * TILE), jnp.bfloat16),
            pltpu.VMEM((16, 16, 2 * TILE), jnp.float32),
        ],
        cost_estimate=pl.CostEstimate(
            flops=1_500_000_000, bytes_accessed=9_000_000, transcendentals=1_000_000
        ),
        compiler_params=pltpu.CompilerParams(vmem_limit_bytes=LIMIT),
        name="attend",
    )(extents, bias, queries, d_out, keys, values, near_row, far_row, near, far)

    piece = exchange(part.reshape(lax.axis_size("col"), -1, TILE), "col")
    d_left, d_right, piece = lax.optimization_barrier((d_left, d_right, piece))
    from_near = swap(jnp.where(even, d_right, d_left), "col", 0)
    from_far = swap(jnp.where(even, d_left, d_right), "col", 1)
    piece = gathered(jnp.sum(piece, 0), "row")
    from_near, from_far, piece = lax.optimization_barrier((from_near, from_far, piece))
    to_near, to_far = pl.pallas_call(
        border_body,
        out_shape=(shape(d_top.shape), shape(d_top.shape)),
        in_specs=[VMEM] * 4,
        out_specs=(VMEM, VMEM),
        compiler_params=pltpu.CompilerParams(vmem_limit_bytes=LIMIT),
        name="border",
    )(d_top, d_bottom, from_near, from_far)
    to_near, to_far, piece = lax.optimization_barrier((to_near, to_far, piece))
    total = gathered(jnp.sum(piece, 0), "col").reshape(part.shape)
    near_row = swap(to_near, "row", 0)
    far_row = swap(to_far, "row", 1)
    d_keys, d_values, d_rel_bias = pl.pallas_call(
        final_body,
        out_shape=(shape(keys.shape), shape(keys.shape), shape(rel_bias.shape, jnp.float32)),
        in_specs=[VMEM] * 6,
        out_specs=(VMEM, VMEM, VMEM),
        compiler_params=pltpu.CompilerParams(vmem_limit_bytes=LIMIT),
        name="final",
    )(own, from_near, from_far, near_row, far_row, total)
    return (attended, d_queries, d_keys, d_values, d_rel_bias)


def solution(mesh):
    tiles = P("row", "col", None)
    return jax.shard_map(
        shards,
        mesh=mesh,
        in_specs=(tiles, tiles, tiles, tiles, P(), P()),
        out_specs=(tiles, tiles, tiles, tiles, P()),
        check_vma=False,
    )
```
